32 devices in a mesh: row: 4 (over y, x), col: 8 (over z, core).
Axes of the slice: x: 2, y: 2, z: 4, core: 2. Of those that a mesh axis runs over, the one named last changes fastest.
Arguments:
- tokens: bfloat16 [512, 16384], P('col', 'row'), may hold values from -6 to 6
- weight: bfloat16 [16384, 32768], P('row', 'col'), may hold values from -0.21875 to 0.21875
- logits: float32 [3, 32768], P(None, 'col'), may hold values from -6 to 303
- cotangent: bfloat16 [512, 32768], P('row', 'col'), may hold values from -6 to 6
Outputs:
- mixed_out: bfloat16 [512, 32768], P('row', 'col')
- input_grad: bfloat16 [512, 16384], P('col', 'row')
- weight_grad: bfloat16 [16384, 32768], P('row', 'col')
- logit_grad: float32 [3, 32768], P(None, 'col')
The draws below stay inside these ranges and needn't reach their ends.
All inputs are finite; a program needn't handle non-finite values.
Results may differ from the reference program's by a relative error of at most 0.0049.
Values may be sent and summed in bfloat16 or wider, within the bound.
No kernel may reach another device: no remote copies, remote signals or barrier semaphores. Data moves between devices by JAX's collectives and lax.ppermute only.
A program may use at most 192 MiB of HBM per device.

```python
import math
import jax
import jax.numpy as jnp
from jax import lax

D = 16384
FF = 32768
TOKENS = 512


def draw_weight(key, part):
    first, second, third = jax.random.split(key, 3)
    base = jnp.clip(jax.random.normal(first, (D, FF), jnp.float32), -4.0, 4.0)
    upper = 10.0
    row_scale = jnp.exp(jax.random.uniform(second, (D, 1), jnp.float32) * jnp.log(upper))
    col_scale = jnp.exp(jax.random.uniform(third, (1, FF), jnp.float32) * jnp.log(upper))
    return (base * row_scale * col_scale / (16.0 * jnp.sqrt(float(D)))).astype(jnp.bfloat16)


def draw_logits(key, part):
    first = jax.random.fold_in(key, 0)
    return jnp.clip(1.5 * jax.random.normal(first, (3, FF), jnp.float32), -6.0, 6.0)


def raised(result, own_key, source, target, shards_of, factor):
    owner, partner = [(jnp.arange(result.shape[position]) // (result.shape[position] // shards_of)).reshape([-1 if axis == position else 1 for axis in range(result.ndim)]) for position in (source, target)]
    chosen = jax.random.permutation(own_key, shards_of)[partner]
    strong = (owner == chosen) | (owner == (partner + shards_of // 2) % shards_of)
    return jnp.where(strong, factor * result, result)


def level_of(key, dims, shards, smallest, high):
    def one(dim, parts):
        heights = jax.random.uniform(jax.random.fold_in(jax.random.fold_in(key, 6), dim), (parts,), jnp.float32, smallest / len(shards), high / len(shards))
        return jnp.repeat(jnp.exp(heights), dims[dim] // parts).reshape((-1,) + (1,) * (len(dims) - dim - 1))

    level = one(*shards[0])
    for cut in shards[1:]:
        level = level * one(*cut)
    return level


def heavy_noise(own_key, dims, scale, reach, cuts, heavy, kind=jnp.bfloat16):
    result = scale * jax.random.normal(own_key, dims, jnp.float32)
    if cuts:
        result = result * level_of(own_key, dims, cuts, -0.22, 0.18)
    return jnp.clip(raised(result, jax.random.fold_in(own_key, 3), *heavy), -reach, reach).astype(kind)


def setup_inputs(seed: int = 0) -> dict:
    seeds = jax.random.split(jax.random.key(seed), 5)
    return {
        "tokens": heavy_noise(seeds[0], (TOKENS, D), 1.0, 6.0, ((0, 8), (1, 4)), (1, 0, 8, 2.0)),
        "weight": draw_weight(jax.random.fold_in(seeds[4], 71), 0),
        "logits": draw_logits(jax.random.fold_in(seeds[4], 71), 0),
        "cotangent": heavy_noise(seeds[3], (TOKENS, FF), 1.0, 6.0, ((0, 4), (1, 8)), (1, 0, 8, 2.0)),
    }


EPSILON = 1e-6
TWO_PI = 2.0 * math.pi
grid_levels = (1.0, 7.0, 127.0)


def quantize(master, peak, scores):
    shares = jax.nn.softmax(scores, axis=0)
    blended = jnp.zeros_like(master)
    slopes = jnp.zeros_like(master)
    candidates = []
    for number, level_value in enumerate(grid_levels):
        spacing = (peak + EPSILON) / level_value
        scaled = master / spacing
        angle_value = TWO_PI * scaled
        candidate = spacing * (scaled - jnp.sin(angle_value) / TWO_PI)
        blended = blended + shares[number] * candidate
        slopes = slopes + shares[number] * (1.0 - jnp.cos(angle_value))
        candidates.append(candidate)
    return shares, blended, slopes, candidates


def logit_slopes(shares, terms):
    return shares * (terms - jnp.sum(shares * terms, axis=0, keepdims=True))


def reference(tokens, weight, logits, cotangent):
    block_width = math.gcd(FF, 1024)
    block_count = FF // block_width

    def advance(running, index_value):
        offset = (index_value * block_width).astype(jnp.int32)
        master = lax.dynamic_slice_in_dim(weight, offset, block_width, 1).astype(jnp.float32)
        scores = lax.dynamic_slice_in_dim(logits, offset, block_width, 1)
        cot_block = lax.dynamic_slice_in_dim(cotangent, offset, block_width, 1)
        peak = jnp.max(jnp.abs(master), axis=0)
        shares, blended, slopes, candidates = quantize(master, peak, scores)
        blend_half = blended.astype(jnp.bfloat16)
        output_block = jnp.dot(tokens, blend_half, preferred_element_type=jnp.float32).astype(jnp.bfloat16)
        running = running + jnp.dot(cot_block, blend_half.T, preferred_element_type=jnp.float32)
        mixed_grad = jnp.dot(tokens.T, cot_block, preferred_element_type=jnp.float32)
        grad_block = (mixed_grad * slopes).astype(jnp.bfloat16)
        terms = jnp.stack([jnp.sum(mixed_grad * candidate, axis=0) for candidate in candidates])
        return running, (output_block, grad_block, logit_slopes(shares, terms))

    start_value = jnp.zeros((TOKENS, D), jnp.float32)
    summed, stacked = lax.scan(advance, start_value, jnp.arange(block_count, dtype=jnp.int32))
    output_blocks, grad_blocks, logit_blocks = stacked
    mixed_out = output_blocks.transpose(1, 0, 2).reshape(TOKENS, FF)
    weight_grad = grad_blocks.transpose(1, 0, 2).reshape(D, FF)
    logit_grad = logit_blocks.transpose(1, 0, 2).reshape(3, FF)
    return mixed_out, summed.astype(jnp.bfloat16), weight_grad, logit_grad
```

```python
import functools
import math

import jax
import jax.numpy as jnp
from jax import lax
from jax.experimental import pallas as pl
from jax.experimental.pallas import tpu as pltpu
from jax.sharding import PartitionSpec as P

EPSILON = 1e-06
TWO_PI = 2.0 * math.pi
LEVELS = (1.0, 7.0, 127.0)
S0, S1, S2, S3 = 6.28316, -10.33428, 5.0838, -1.1093


def main_kernel(meta, *refs, nrow, ncol, nd, nj, bd, bj, strip):
    nz = ncol // 2
    it = iter(refs)
    take = lambda n: [next(it) for _ in range(n)]
    tok_in, cot_in = take(ncol), take(nrow)
    w_ref, const_ref = take(2)
    wg_ref, terms_ref = take(2)
    out_refs, keep_refs, send_refs = take(nrow), take(nz), take(nz)
    tok, tokt, cot, out_acc, in_acc, bl, mg, sems = take(8)
    jn, dn = pl.program_id(0), pl.program_id(1)
    row, col = meta[0], meta[1]
    rows_t, rows_c = tok_in[0].shape[0], cot_in[0].shape[0]

    @pl.when((jn == 0) & (dn == 0))
    def _():
        copies = []
        for k in range(nrow):
            off = pl.multiple_of((row ^ k) * rows_c, rows_c)
            copies.append(pltpu.make_async_copy(cot_in[k], cot.at[pl.ds(off, rows_c), :], sems.at[k]))
        for k in range(ncol):
            off = pl.multiple_of((col ^ k) * rows_t, rows_t)
            copies.append(
                pltpu.make_async_copy(tok_in[k], tok.at[pl.ds(off, rows_t), :], sems.at[nrow + k])
            )
        for copy in copies:
            copy.start()
        in_acc[...] = jnp.zeros_like(in_acc)
        for copy in copies:
            copy.wait()
        for n in range(nd):
            tokt[n] = tok[:, n * bd : (n + 1) * bd].T

    @pl.when(dn == 0)
    def _():
        out_acc[...] = jnp.zeros_like(out_acc)
        terms_ref[...] = jnp.zeros_like(terms_ref)

    cot_j = cot[:, pl.ds(pl.multiple_of(jn * bj, bj), bj)]
    mg[...] = jnp.dot(tokt[dn], cot_j, preferred_element_type=jnp.float32)
    for lane in range(0, bj, 128):
        cols = slice(lane, lane + 128)
        inv0, inv2, k0, k1, k2, h0, h1, h2 = [const_ref[n : n + 1, cols] for n in range(8)]
        sums = [jnp.zeros((8, 128), jnp.float32) for _ in range(4)]
        for top in range(0, bd, strip):
            part = slice(top, top + strip)
            w = w_ref[part, cols].astype(jnp.float32)
            g = mg[part, cols]
            r = w * inv0
            f = r - jnp.round(r)
            y = f * f
            s = (((S3 * y + S2) * y + S1) * y + S0) * f
            x = s * s
            q = jnp.maximum(4.0 - x, 1e-30)
            a0 = s * (q * lax.rsqrt(q))
            v = 2.0 - x
            z = v * v
            e = z - 1.0
            o = v * (z - 2.0)
            up, dn_ = o + e, o - e
            pq = up * dn_
            u = w * inv2
            f2 = u - jnp.round(u)
            y2 = f2 * f2
            s2 = (((y2 + S2 / S3) * y2 + S1 / S3) * y2 + S0 / S3) * f2
            x2 = s2 * s2
            q2 = jnp.maximum(4.0 / (S3 * S3) - x2, 1e-30)
            a2 = s2 * (q2 * lax.rsqrt(q2))
            blend = w - a0 * (k0 + k1 * pq) - k2 * a2
            slope = x * (h0 + h1 * (up * up)) + h2 * x2
            bl[part, cols] = blend.astype(jnp.bfloat16)
            wg_ref[part, cols] = (g * slope).astype(jnp.bfloat16)
            m0 = g * a0
            for n, val in enumerate((m0, m0 * pq, g * a2, g * w)):
                sums[n] = sums[n] + val.reshape(strip // 8, 8, 128).sum(0)
        for n in range(4):
            terms_ref[n, :, cols] += sums[n]
    blv = bl[...]
    tok_d = tok[:, pl.ds(pl.multiple_of(dn * bd, bd), bd)]
    out_acc[...] += jnp.dot(tok_d, blv, preferred_element_type=jnp.float32)
    in_acc[dn] += lax.dot_general(
        cot_j, blv, (((1,), (1,)), ((), ())), preferred_element_type=jnp.float32
    )

    @pl.when(dn == nd - 1)
    def _():
        for k in range(nrow):
            off = pl.multiple_of((row ^ k) * rows_c, rows_c)
            out_refs[k][...] = out_acc[pl.ds(off, rows_c), :].astype(jnp.bfloat16)

    @pl.when(jn == nj - 1)
    def _():
        core = col & 1
        for k in range(nz):
            base = ((col >> 1) ^ k) * 2
            mine = pl.multiple_of((base + core) * rows_t, rows_t)
            other = pl.multiple_of((base + 1 - core) * rows_t, rows_t)
            keep_refs[k][...] = in_acc[dn, pl.ds(mine, rows_t), :].astype(jnp.bfloat16)
            send_refs[k][...] = in_acc[dn, pl.ds(other, rows_t), :].astype(jnp.bfloat16)


def main_call(meta, toks, cots, weight, consts, *, bd=256, bj=512, strip=64):
    nrow, ncol = len(cots), len(toks)
    nz = ncol // 2
    depth, width = weight.shape
    bd, bj = min(bd, depth), min(bj, width)
    nd, nj = depth // bd, width // bj
    rows_t, rows_c = toks[0].shape[0], cots[0].shape[0]
    tokens = rows_t * ncol
    last = lambda j, d, m: (0, jnp.where(j == nj - 1, d, 0))
    bf = jnp.bfloat16
    hbm = pl.BlockSpec(memory_space=pl.ANY)
    grid_spec = pltpu.PrefetchScalarGridSpec(
        num_scalar_prefetch=1,
        grid=(nj, nd),
        in_specs=[hbm] * (nrow + ncol)
        + [
            pl.BlockSpec((bd, bj), lambda j, d, m: (d, j)),
            pl.BlockSpec((8, bj), lambda j, d, m: (0, j)),
        ],
        out_specs=[
            pl.BlockSpec((bd, bj), lambda j, d, m: (d, j)),
            pl.BlockSpec((4, 8, bj), lambda j, d, m: (0, 0, j)),
        ]
        + [pl.BlockSpec((rows_c, bj), lambda j, d, m: (0, j))] * nrow
        + [pl.BlockSpec((rows_t, bd), last)] * (2 * nz),
        scratch_shapes=[
            pltpu.VMEM((tokens, depth), bf),
            pltpu.VMEM((nd, bd, tokens), bf),
            pltpu.VMEM((tokens, width), bf),
            pltpu.VMEM((tokens, bj), jnp.float32),
            pltpu.VMEM((nd, tokens, bd), jnp.float32),
            pltpu.VMEM((bd, bj), bf),
            pltpu.VMEM((bd, bj), jnp.float32),
            pltpu.SemaphoreType.DMA((nrow + ncol,)),
        ],
    )
    shape = jax.ShapeDtypeStruct
    res = pl.pallas_call(
        functools.partial(
            main_kernel, nrow=nrow, ncol=ncol, nd=nd, nj=nj, bd=bd, bj=bj, strip=strip
        ),
        grid_spec=grid_spec,
        out_shape=[shape((depth, width), bf), shape((4, 8, width), jnp.float32)]
        + [shape((rows_c, width), bf)] * nrow
        + [shape((rows_t, depth), bf)] * (2 * nz),
        compiler_params=pltpu.CompilerParams(vmem_limit_bytes=60 * 1024 * 1024),
        cost_estimate=pl.CostEstimate(
            flops=6 * depth * width * tokens,
            bytes_accessed=4 * depth * width,
            transcendentals=2 * depth * width,
        ),
        name="main_kernel",
    )(meta, *toks, *cots, weight, consts)
    wg, terms = res[:2]
    outs = res[2 : 2 + nrow]
    keeps = res[2 + nrow : 2 + nrow + nz]
    sends = res[2 + nrow + nz :]
    return wg, terms, outs, keeps, sends


def swap(value, axis, size, k):
    return lax.ppermute(value, axis, [(i, i ^ k) for i in range(size)])


def shards(nrow, ncol, tokens, weight, logits, cotangent):
    nz = ncol // 2
    f32 = jnp.float32
    cots = [cotangent] + [swap(cotangent, "row", nrow, k) for k in range(1, nrow)]
    even = [tokens] + [swap(tokens, "col", ncol, 2 * k) for k in range(1, nz)]
    toks = []
    for t in even:
        toks += [t, swap(t, "col", ncol, 1)]
    peak = jnp.max(jnp.abs(weight), axis=0, keepdims=True).astype(f32)
    for other in [swap(peak, "row", nrow, k) for k in range(1, nrow)]:
        peak = jnp.maximum(peak, other)
    shares = jax.nn.softmax(logits, axis=0)
    spacing = [(peak + EPSILON) / level for level in LEVELS]
    scale = [sp / (2.0 * TWO_PI) for sp in spacing]
    fold = S3 * S3
    consts = jnp.concatenate(
        [
            1.0 / spacing[0],
            1.0 / spacing[2],
            shares[0:1] * scale[0],
            shares[1:2] * scale[1],
            shares[2:3] * scale[2] * -fold,
            shares[0:1] * 0.5,
            shares[1:2] * 0.5,
            shares[2:3] * (0.5 * fold),
        ],
        axis=0,
    )
    meta = jnp.stack([lax.axis_index("row"), lax.axis_index("col")]).astype(jnp.int32)
    wg, parts, outs, keeps, sends = main_call(meta, toks, cots, weight, consts)

    got = [swap(sends[k], "col", ncol, 1) for k in range(nz)]
    sums = [keeps[k].astype(f32) + got[k].astype(f32) for k in range(nz)]
    far = [swap(sums[k].astype(jnp.bfloat16), "col", ncol, 2 * k) for k in range(1, nz)]
    input_grad = sum([sums[0]] + [x.astype(f32) for x in far]).astype(jnp.bfloat16)

    far = [swap(outs[k], "row", nrow, k) for k in range(1, nrow)]
    mixed_out = sum([outs[0].astype(f32)] + [x.astype(f32) for x in far]).astype(jnp.bfloat16)

    parts = parts.sum(1)
    common = parts[3:4]
    terms = jnp.concatenate(
        [
            common - scale[0] * parts[0:1],
            common - scale[1] * parts[1:2],
            common + (scale[2] * fold) * parts[2:3],
        ],
        axis=0,
    )
    terms = sum([terms] + [swap(terms, "row", nrow, k) for k in range(1, nrow)])
    logit_grad = shares * (terms - jnp.sum(shares * terms, axis=0, keepdims=True))
    return mixed_out, input_grad, wg, logit_grad


def solution(mesh):
    in_specs = (P("col", "row"), P("row", "col"), P(None, "col"), P("row", "col"))
    out_specs = (P("row", "col"), P("col", "row"), P("row", "col"), P(None, "col"))
    body = functools.partial(shards, mesh.shape["row"], mesh.shape["col"])
    return jax.shard_map(body, mesh=mesh, in_specs=in_specs, out_specs=out_specs, check_vma=False)
```

```python
import functools
import math

import jax
import jax.numpy as jnp
from jax import lax
from jax.experimental import pallas as pl
from jax.experimental.pallas import tpu as pltpu
from jax.sharding import PartitionSpec as P


EPSILON = 1e-06
TWO_PI = 2.0 * math.pi
LEVELS = (1.0, 7.0, 127.0)
S0, S1, S2, S3 = 6.28312416, -10.3332539, 5.07633545, -1.09334416
FOLD = S3 * S3


def main_kernel(meta, *refs, nrow, ncol, nd, nj, bd, bj, strip, d0, t0, j0, carry_out, last_out, carry_in):
    nz = ncol // 2
    it = iter(refs)
    take = lambda n: [next(it) for _ in range(n)]
    tok_in, cot_in = take(ncol), take(nrow)
    w_ref, const_ref = take(2)
    take(1 if d0 or j0 else 0)
    out_prev = take(1)[0] if carry_out else None
    in_prev = take(1)[0] if j0 else None
    wg_ref, terms_ref = take(2)
    outs = take(nrow + 1) if last_out else take(1)
    ins = take(1) if carry_in else take(2)
    tok, tokt, cot, out_acc, in_acc, terms, bl_a, bl_b, mg_a, mg_b, sems, sem_out = take(12)
    dn, jn = pl.program_id(0), pl.program_id(1)
    row, col = meta[0], meta[1]
    rows_t, rows_c = tok_in[0].shape[0], cot_in[0].shape[0]
    step = dn * nj + jn
    wide = min(256, bj)

    def prev_copy(tile):
        return pltpu.make_async_copy(
            out_prev.at[j0 // bj + tile], out_acc.at[tile], sem_out.at[tile]
        )

    def out_copy(tile):
        return pltpu.make_async_copy(out_acc.at[tile], outs[0].at[tile], sem_out.at[tile])

    tokens = cot.shape[1]

    def gradient(d, tile, mg):
        def piece(cols):
            mg[:, cols] = jnp.dot(tokt[d], cot[tile, :, cols], preferred_element_type=jnp.float32)

        return [functools.partial(piece, slice(n, n + wide)) for n in range(0, bj, wide)]

    def products(d, tile, bl):
        def out_piece(cols):
            out_acc[tile, :, cols] += jnp.dot(tok[d], bl[:, cols], preferred_element_type=jnp.float32)

        def in_piece(part):
            in_acc[d, part, :] += lax.dot_general(
                cot[tile, part, :], bl[...], (((1,), (1,)), ((), ())), preferred_element_type=jnp.float32
            )

        half = tokens // 2
        outs = [functools.partial(out_piece, slice(n, n + wide)) for n in range(0, bj, wide)]
        return outs + [functools.partial(in_piece, slice(n, n + half)) for n in range(0, tokens, half)]

    @pl.when(step == 0)
    def _():
        copies = []
        for k in range(nrow):
            off = pl.multiple_of((row ^ k) * rows_c, rows_c)
            for n in range(2 * nj):
                src = cot_in[k].at[:, j0 + n * bj : j0 + (n + 1) * bj]
                dst = cot.at[n, pl.ds(off, rows_c), :]
                copies.append(pltpu.make_async_copy(src, dst, sems.at[len(copies)]))
        for k in range(ncol):
            off = pl.multiple_of((col ^ k) * rows_t, rows_t)
            for n in range(nd):
                src = tok_in[k].at[:, t0 + n * bd : t0 + (n + 1) * bd]
                dst = tok.at[n, pl.ds(off, rows_t), :]
                copies.append(pltpu.make_async_copy(src, dst, sems.at[len(copies)]))
        if in_prev is not None:
            copies.append(pltpu.make_async_copy(in_prev, in_acc, sems.at[len(copies)]))
        for copy in copies:
            copy.start()
        if carry_out:
            for tile in range(2 * nj):
                prev_copy(tile).start()
        else:

            @pl.loop(0, 2 * nj)
            def _(tile):
                out_acc[tile] = jnp.zeros(out_acc.shape[1:], jnp.float32)

        if in_prev is None:

            @pl.loop(0, nd)
            def _(d):
                in_acc[d] = jnp.zeros(in_acc.shape[1:], jnp.float32)

        terms[...] = jnp.zeros_like(terms)
        bl_b[...] = jnp.zeros_like(bl_b)
        for copy in copies:
            copy.wait()

        @pl.loop(0, nd)
        def _(d):
            tokt[d] = tok[d].T

        for piece in gradient(0, 0, mg_a):
            piece()

    if carry_out:

        @pl.when(dn == 0)
        def _():
            prev_copy(2 * jn).wait()
            prev_copy(2 * jn + 1).wait()

    def strips(mg, bl, left, lane, tops):
        here = slice(lane, lane + 128)
        cols = slice(left + lane, left + lane + 128)
        inv0, inv2, k0, k1, k2, h0, h1, h2 = [const_ref[n : n + 1, cols] for n in range(8)]
        sums = [None] * 3
        for top in tops:
            part = slice(top, top + strip)
            w = w_ref[part, cols].astype(jnp.float32)
            g = mg[part, here]
            r = w * inv0
            f = r - jnp.round(r)
            y = f * f
            s = (((S3 * y + S2) * y + S1) * y + S0) * f
            x = s * s
            q = 4.0 - x
            a0 = s * (q * lax.rsqrt(q))
            v = 2.0 - x
            z = v * v
            e = z - 1.0
            o = v * (z - 2.0)
            up, down = o + e, o - e
            pq = up * down
            u = w * inv2
            f2 = u - jnp.round(u)
            y2 = f2 * f2
            s2 = (((y2 + S2 / S3) * y2 + S1 / S3) * y2 + S0 / S3) * f2
            x2 = s2 * s2
            q2 = 4.0 / FOLD - x2
            a2 = s2 * (q2 * lax.rsqrt(q2))
            blend = w - a0 * (k0 + k1 * pq) - k2 * a2
            slope = x * (h0 + h1 * (up * up)) + h2 * x2
            bl[part, here] = blend.astype(jnp.bfloat16)
            wg_ref[part, cols] = (g * slope).astype(jnp.bfloat16)
            m0 = g * a0
            for n, val in enumerate((m0, m0 * pq, g * a2)):
                val = val.reshape(strip // 8, 8, 128).sum(0)
                sums[n] = val if sums[n] is None else sums[n] + val
        return sums

    def arithmetic(mg, bl, tile, left, beside):
        n_blocks = bj // 128
        for n in range(n_blocks):
            share = beside[n * len(beside) // n_blocks : (n + 1) * len(beside) // n_blocks]

            @pl.when(step >= 0)
            def _(n=n, share=share):
                lane = n * 128
                for piece in share:
                    piece()
                sums = strips(mg, bl, left, lane, range(0, bd, strip))
                for m in range(3):
                    terms[tile, m, :, lane : lane + 128] += sums[m]

    before = jnp.maximum(step - 1, 0)
    after = jnp.minimum(step + 1, nd * nj - 1)
    left, right = 2 * jn, 2 * jn + 1
    arithmetic(
        mg_a, bl_a, left, 0, gradient(dn, right, mg_b) + products(before // nj, 2 * (before % nj) + 1, bl_b)
    )
    arithmetic(
        mg_b, bl_b, right, bj, gradient(after // nj, 2 * (after % nj), mg_a) + products(dn, left, bl_a)
    )

    @pl.when(step == nd * nj - 1)
    def _():
        for piece in products(nd - 1, 2 * nj - 1, bl_b):
            piece()
        for tile in range(2 * nj):
            for n in range(3):
                terms_ref[n : n + 1, tile * bj : (tile + 1) * bj] = terms[tile, n].sum(0, keepdims=True)

    if last_out:

        @pl.when(step == nd * nj - 1)
        def _():
            for tile in range(2 * nj):
                cols = slice(tile * bj, (tile + 1) * bj)
                for k in range(nrow):
                    off = pl.multiple_of((row ^ k) * rows_c, rows_c)
                    outs[k][:, cols] = out_acc[tile, pl.ds(off, rows_c), :].astype(jnp.bfloat16)
                total = jnp.zeros((8, bj), jnp.float32)
                for top in range(0, tokens, 32):
                    val = out_acc[tile, top : top + 32, :] * cot[tile, top : top + 32, :].astype(jnp.float32)
                    total = total + val.reshape(4, 8, bj).sum(0)
                outs[nrow][:, cols] = total.sum(0, keepdims=True)

    else:

        @pl.when(dn == nd - 1)
        def _():
            out_copy(left).start()

        @pl.when((dn == nd - 1) & (jn > 0))
        def _():
            out_copy(left - 1).start()

        @pl.when(step == nd * nj - 1)
        def _():
            out_copy(2 * nj - 1).start()
            for tile in range(2 * nj):
                out_copy(tile).wait()

    @pl.when(step == nd * nj - 1)
    def _():
        if carry_in:
            ins[0][...] = in_acc[...]
        else:
            core = col & 1
            for d in range(nd):
                cols = slice(d * bd, (d + 1) * bd)
                for k in range(nz):
                    base = ((col >> 1) ^ k) * 2
                    mine = pl.multiple_of((base + core) * rows_t, rows_t)
                    other = pl.multiple_of((base + 1 - core) * rows_t, rows_t)
                    ins[0][k, :, cols] = in_acc[d, pl.ds(mine, rows_t), :]
                    ins[1][k, :, cols] = in_acc[d, pl.ds(other, rows_t), :].astype(jnp.bfloat16)


def main_call(meta, toks, cots, weight, consts, wg, out_prev, in_prev, *, rows, t0, cols, final, bd=256, bj=512, strip=16):
    nrow, ncol = len(cots), len(toks)
    nz = ncol // 2
    (d0, depth), (j0, width) = rows, cols
    bd, bj = min(bd, depth), min(bj, weight.shape[1] // 4)
    nd, nj = depth // bd, width // (2 * bj)
    rows_t, rows_c = toks[0].shape[0], cots[0].shape[0]
    tokens = rows_t * ncol
    carry_in = j0 + width < weight.shape[1]
    bf, f32 = jnp.bfloat16, jnp.float32
    hbm = pl.BlockSpec(memory_space=pl.ANY)
    tile_at = lambda d, j, m: (d0 // bd + d, j0 // (2 * bj) + j)
    shape = jax.ShapeDtypeStruct

    def whole(dims, kind):
        return pl.BlockSpec(dims, lambda d, j, m, n=len(dims): (0,) * n), shape(dims, kind)

    extra = [x for x in (wg, out_prev, in_prev) if x is not None]
    outs = [
        (pl.BlockSpec((bd, 2 * bj), tile_at), shape(weight.shape, bf)),
        whole((3, width), f32),
    ]
    if final:
        outs += [whole((rows_c, width), bf)] * nrow + [whole((1, width), f32)]
    else:
        outs += [(hbm, shape((2 * nj, tokens, bj), f32))]
    if carry_in:
        outs += [whole((nd, tokens, bd), f32)]
    else:
        outs += [whole((nz, rows_t, depth), f32), whole((nz, rows_t, depth), bf)]
    n_in = 1 + ncol + nrow + 2
    grid_spec = pltpu.PrefetchScalarGridSpec(
        num_scalar_prefetch=1,
        grid=(nd, nj),
        in_specs=[hbm] * (nrow + ncol)
        + [
            pl.BlockSpec((bd, 2 * bj), tile_at),
            pl.BlockSpec((8, 2 * bj), lambda d, j, m: (0, j0 // (2 * bj) + j)),
        ]
        + [hbm] * len(extra),
        out_specs=[spec for spec, _ in outs],
        scratch_shapes=[
            pltpu.VMEM((nd, tokens, bd), bf),
            pltpu.VMEM((nd, bd, tokens), bf),
            pltpu.VMEM((2 * nj, tokens, bj), bf),
            pltpu.VMEM((2 * nj, tokens, bj), f32),
            pltpu.VMEM((nd, tokens, bd), f32),
            pltpu.VMEM((2 * nj, 3, 8, bj), f32),
            pltpu.VMEM((bd, bj), bf),
            pltpu.VMEM((bd, bj), bf),
            pltpu.VMEM((bd, bj), f32),
            pltpu.VMEM((bd, bj), f32),
            pltpu.SemaphoreType.DMA((2 * nj * nrow + nd * ncol + 1,)),
            pltpu.SemaphoreType.DMA((2 * nj,)),
        ],
    )
    return pl.pallas_call(
        functools.partial(
            main_kernel, nrow=nrow, ncol=ncol, nd=nd, nj=nj, bd=bd, bj=bj, strip=strip, d0=d0, t0=t0,
            j0=j0, carry_out=out_prev is not None, last_out=final, carry_in=carry_in,
        ),
        grid_spec=grid_spec,
        out_shape=[out for _, out in outs],
        input_output_aliases={} if wg is None else {n_in: 0},
        compiler_params=pltpu.CompilerParams(vmem_limit_bytes=63 * 1024 * 1024),
        cost_estimate=pl.CostEstimate(
            flops=20 * depth * width * tokens,
            bytes_accessed=4 * depth * width,
            transcendentals=2 * depth * width,
        ),
        name="main_kernel",
    )(meta, *toks, *cots, weight, consts, *extra)


def swap(value, axis, size, k):
    return lax.ppermute(value, axis, [(i, i ^ k) for i in range(size)])


def gather_cotangent(nrow, mine):
    if nrow != 4:
        return [mine] + [swap(mine, "row", nrow, k) for k in range(1, nrow)]
    one, two = [swap(mine, "row", nrow, k) for k in (1, 2)]
    half = mine.shape[0] // 2
    far = [swap(two[:half], "row", nrow, 1), swap(one[half:], "row", nrow, 2)]
    return [mine, one, two, jnp.concatenate(far, axis=0)]


def layer(nrow, ncol, tokens, weight, logits, cotangent):
    nz = ncol // 2
    f32, bf = jnp.float32, jnp.bfloat16
    depth, width = weight.shape
    cut = depth // 4

    def gather_tokens(t):
        toks = []
        for t in [t] + [swap(t, "col", ncol, 2 * k) for k in range(1, nz)]:
            toks += [t, swap(t, "col", ncol, 1)]
        return toks

    first = gather_tokens(tokens[:, :cut])
    cots = gather_cotangent(nrow, cotangent)
    rest = gather_tokens(tokens[:, cut:])
    peak = jnp.max(jnp.abs(weight), axis=0, keepdims=True).astype(f32)
    for other in [swap(peak, "row", nrow, k) for k in range(1, nrow)]:
        peak = jnp.maximum(peak, other)
    shares = jax.nn.softmax(logits, axis=0)
    spacing = [(peak + EPSILON) / level for level in LEVELS]
    scale = [spacing[n] / (2.0 * TWO_PI) * (1.0, 1.0, -FOLD)[n] for n in range(3)]
    consts = jnp.concatenate(
        [1.0 / spacing[0], 1.0 / spacing[2]]
        + [shares[n : n + 1] * scale[n] for n in range(3)]
        + [shares[0:1] * 0.5, shares[1:2] * 0.5, shares[2:3] * (0.5 * FOLD)],
        axis=0,
    )
    meta = jnp.stack([lax.axis_index("row"), lax.axis_index("col")]).astype(jnp.int32)

    calls = [
        (first, (0, cut), 0, (0, width), False),
        (rest, (cut, 2 * cut), 0, (0, width), False),
        (rest, (3 * cut, cut), 2 * cut, (0, width // 2), True),
        (rest, (3 * cut, cut), 2 * cut, (width // 2, width // 2), True),
    ]
    wg = out_prev = in_prev = None
    parts, commons, mixed, inputs = [], [], [], []
    for toks, rows, t0, cols, final in calls:
        wg, part, *res = main_call(
            meta, toks, cots, weight, consts, wg, out_prev, in_prev, rows=rows, t0=t0, cols=cols, final=final
        )
        parts.append(part)
        if final:
            outs, common, res = res[:nrow], res[nrow], res[nrow + 1 :]
            commons.append(common)
            far = [swap(outs[k], "row", nrow, k) for k in range(1, nrow)]
            mixed.append(sum([outs[0].astype(f32)] + [x.astype(f32) for x in far]).astype(bf))
        else:
            out_prev, res = res[0], res[1:]
        if cols[0] + cols[1] < width:
            in_prev = res[0]
        else:
            keep, send = res
            got = swap(send, "col", ncol, 1)
            sums = [keep[k] + got[k].astype(f32) for k in range(nz)]
            far = [swap(sums[k].astype(bf), "col", ncol, 2 * k) for k in range(1, nz)]
            inputs.append(sum([sums[0]] + [x.astype(f32) for x in far]).astype(bf))
    mixed_out = jnp.concatenate(mixed, axis=1)
    input_grad = jnp.concatenate(inputs, axis=1)

    parts = parts[0] + parts[1] + jnp.concatenate(parts[2:], axis=1)
    sines = jnp.concatenate([scale[n] * parts[n : n + 1] for n in range(3)], axis=0)
    common = jnp.concatenate(commons, axis=1) + jnp.sum(shares * sines, axis=0, keepdims=True)
    terms = common - sines
    terms = sum([terms] + [swap(terms, "row", nrow, k) for k in range(1, nrow)])
    logit_grad = shares * (terms - jnp.sum(shares * terms, axis=0, keepdims=True))
    return mixed_out, input_grad, wg, logit_grad


def solution(mesh):
    in_specs = (P("col", "row"), P("row", "col"), P(None, "col"), P("row", "col"))
    out_specs = (P("row", "col"), P("col", "row"), P("row", "col"), P(None, "col"))
    nrow, ncol = mesh.shape["row"], mesh.shape["col"]
    body = functools.partial(layer, nrow, ncol)
    return jax.shard_map(body, mesh=mesh, in_specs=in_specs, out_specs=out_specs, check_vma=False)
```

```python
import functools
import math

import jax
import jax.numpy as jnp
from jax import lax
from jax.experimental import pallas as pl
from jax.experimental.pallas import tpu as pltpu
from jax.sharding import PartitionSpec as P


EPSILON = 1e-06
TWO_PI = 2.0 * math.pi
LEVELS = (1.0, 7.0, 127.0)
S0, S1, S2, S3 = 6.28312416, -10.3332539, 5.07633545, -1.09334416
FOLD = S3 * S3


def main_kernel(meta, *refs, nrow, ncol, nd, nj, bd, bj, strip, d0, t0, j0, carry_out, last_out, carry_in):
    nz = ncol // 2
    it = iter(refs)
    take = lambda n: [next(it) for _ in range(n)]
    tok_in, cot_in = take(ncol), take(nrow)
    w_ref, const_ref = take(2)
    take(1 if d0 or j0 else 0)
    out_prev = take(1)[0] if carry_out else None
    in_prev = take(1)[0] if j0 else None
    wg_ref, terms_ref = take(2)
    outs = take(nrow + 1) if last_out else take(1)
    ins = take(1) if carry_in else take(2)
    tok, tokt, cot, out_acc, in_acc, terms, bl_a, bl_b, mg_a, mg_b, sems, sem_out = take(12)
    dn, jn = pl.program_id(0), pl.program_id(1)
    row, col = meta[0], meta[1]
    rows_t, rows_c = tok_in[0].shape[0], cot_in[0].shape[0]
    step = dn * nj + jn
    wide = min(256, bj)

    def prev_copy(tile):
        return pltpu.make_async_copy(
            out_prev.at[j0 // bj + tile], out_acc.at[tile], sem_out.at[tile]
        )

    def out_copy(tile):
        return pltpu.make_async_copy(out_acc.at[tile], outs[0].at[tile], sem_out.at[tile])

    tokens = cot.shape[1]

    def gradient(d, tile, mg):
        def piece(cols):
            mg[:, cols] = jnp.dot(tokt[d], cot[tile, :, cols], preferred_element_type=jnp.float32)

        return [functools.partial(piece, slice(n, n + wide)) for n in range(0, bj, wide)]

    def products(d, tile, bl):
        def out_piece(cols):
            out_acc[tile, :, cols] += jnp.dot(tok[d], bl[:, cols], preferred_element_type=jnp.float32)

        def in_piece(part):
            in_acc[d, part, :] += lax.dot_general(
                cot[tile, part, :], bl[...], (((1,), (1,)), ((), ())), preferred_element_type=jnp.float32
            )

        half = tokens // 2
        outs = [functools.partial(out_piece, slice(n, n + wide)) for n in range(0, bj, wide)]
        return outs + [functools.partial(in_piece, slice(n, n + half)) for n in range(0, tokens, half)]

    @pl.when(step == 0)
    def _():
        copies = []
        for k in range(nrow):
            off = pl.multiple_of((row ^ k) * rows_c, rows_c)
            for n in range(2 * nj):
                src = cot_in[k].at[:, j0 + n * bj : j0 + (n + 1) * bj]
                dst = cot.at[n, pl.ds(off, rows_c), :]
                copies.append(pltpu.make_async_copy(src, dst, sems.at[len(copies)]))
        for k in range(ncol):
            off = pl.multiple_of((col ^ k) * rows_t, rows_t)
            for n in range(nd):
                src = tok_in[k].at[:, t0 + n * bd : t0 + (n + 1) * bd]
                dst = tok.at[n, pl.ds(off, rows_t), :]
                copies.append(pltpu.make_async_copy(src, dst, sems.at[len(copies)]))
        if in_prev is not None:
            copies.append(pltpu.make_async_copy(in_prev, in_acc, sems.at[len(copies)]))
        for copy in copies:
            copy.start()
        if carry_out:
            for tile in range(2 * nj):
                prev_copy(tile).start()
        else:

            @pl.loop(0, 2 * nj)
            def _(tile):
                out_acc[tile] = jnp.zeros(out_acc.shape[1:], jnp.float32)

        if in_prev is None:

            @pl.loop(0, nd)
            def _(d):
                in_acc[d] = jnp.zeros(in_acc.shape[1:], jnp.float32)

        terms[...] = jnp.zeros_like(terms)
        bl_b[...] = jnp.zeros_like(bl_b)
        for copy in copies:
            copy.wait()

        @pl.loop(0, nd)
        def _(d):
            tokt[d] = tok[d].T

        for piece in gradient(0, 0, mg_a):
            piece()

    if carry_out:

        @pl.when(dn == 0)
        def _():
            prev_copy(2 * jn).wait()
            prev_copy(2 * jn + 1).wait()

    def strips(mg, bl, left, lane, tops):
        here = slice(lane, lane + 128)
        cols = slice(left + lane, left + lane + 128)
        inv0, inv2, k0, k1, k2, h0, h1, h2 = [const_ref[n : n + 1, cols] for n in range(8)]
        sums = [None] * 3
        for top in tops:
            part = slice(top, top + strip)
            w = w_ref[part, cols].astype(jnp.float32)
            g = mg[part, here]
            r = w * inv0
            f = r - jnp.round(r)
            y = f * f
            s = (((S3 * y + S2) * y + S1) * y + S0) * f
            x = s * s
            q = 4.0 - x
            a0 = s * (q * lax.rsqrt(q))
            v = 2.0 - x
            z = v * v
            e = z - 1.0
            o = v * (z - 2.0)
            up, down = o + e, o - e
            pq = up * down
            u = w * inv2
            f2 = u - jnp.round(u)
            y2 = f2 * f2
            s2 = (((y2 + S2 / S3) * y2 + S1 / S3) * y2 + S0 / S3) * f2
            x2 = s2 * s2
            q2 = 4.0 / FOLD - x2
            a2 = s2 * (q2 * lax.rsqrt(q2))
            blend = w - a0 * (k0 + k1 * pq) - k2 * a2
            slope = x * (h0 + h1 * (up * up)) + h2 * x2
            bl[part, here] = blend.astype(jnp.bfloat16)
            wg_ref[part, cols] = (g * slope).astype(jnp.bfloat16)
            m0 = g * a0
            for n, val in enumerate((m0, m0 * pq, g * a2)):
                val = val.reshape(strip // 8, 8, 128).sum(0)
                sums[n] = val if sums[n] is None else sums[n] + val
        return sums

    def arithmetic(mg, bl, tile, left, beside):
        n_blocks = bj // 128
        for n in range(n_blocks):
            share = beside[n * len(beside) // n_blocks : (n + 1) * len(beside) // n_blocks]

            @pl.when(step >= 0)
            def _(n=n, share=share):
                lane = n * 128
                for piece in share:
                    piece()
                sums = strips(mg, bl, left, lane, range(0, bd, strip))
                for m in range(3):
                    terms[tile, m, :, lane : lane + 128] += sums[m]

    before = jnp.maximum(step - 1, 0)
    after = jnp.minimum(step + 1, nd * nj - 1)
    left, right = 2 * jn, 2 * jn + 1
    arithmetic(
        mg_a, bl_a, left, 0, gradient(dn, right, mg_b) + products(before // nj, 2 * (before % nj) + 1, bl_b)
    )
    arithmetic(
        mg_b, bl_b, right, bj, gradient(after // nj, 2 * (after % nj), mg_a) + products(dn, left, bl_a)
    )

    @pl.when(step == nd * nj - 1)
    def _():
        for piece in products(nd - 1, 2 * nj - 1, bl_b):
            piece()
        for tile in range(2 * nj):
            for n in range(3):
                terms_ref[n : n + 1, tile * bj : (tile + 1) * bj] = terms[tile, n].sum(0, keepdims=True)

    if last_out:

        @pl.when(step == nd * nj - 1)
        def _():
            for tile in range(2 * nj):
                cols = slice(tile * bj, (tile + 1) * bj)
                for k in range(nrow):
                    off = pl.multiple_of((row ^ k) * rows_c, rows_c)
                    outs[k][:, cols] = out_acc[tile, pl.ds(off, rows_c), :].astype(jnp.bfloat16)
                total = jnp.zeros((8, bj), jnp.float32)
                for top in range(0, tokens, 32):
                    val = out_acc[tile, top : top + 32, :] * cot[tile, top : top + 32, :].astype(jnp.float32)
                    total = total + val.reshape(4, 8, bj).sum(0)
                outs[nrow][:, cols] = total.sum(0, keepdims=True)

    else:

        @pl.when(dn == nd - 1)
        def _():
            out_copy(left).start()

        @pl.when((dn == nd - 1) & (jn > 0))
        def _():
            out_copy(left - 1).start()

        @pl.when(step == nd * nj - 1)
        def _():
            out_copy(2 * nj - 1).start()
            for tile in range(2 * nj):
                out_copy(tile).wait()

    @pl.when(step == nd * nj - 1)
    def _():
        if carry_in:
            ins[0][...] = in_acc[...]
        else:
            core = col & 1
            for d in range(nd):
                cols = slice(d * bd, (d + 1) * bd)
                for k in range(nz):
                    base = ((col >> 1) ^ k) * 2
                    mine = pl.multiple_of((base + core) * rows_t, rows_t)
                    other = pl.multiple_of((base + 1 - core) * rows_t, rows_t)
                    ins[0][k, :, cols] = in_acc[d, pl.ds(mine, rows_t), :]
                    ins[1][k, :, cols] = in_acc[d, pl.ds(other, rows_t), :].astype(jnp.bfloat16)


def main_call(meta, toks, cots, weight, consts, wg, out_prev, in_prev, *, rows, t0, cols, final, bd=512, bj=512, strip=32):
    nrow, ncol = len(cots), len(toks)
    nz = ncol // 2
    (d0, depth), (j0, width) = rows, cols
    bd, bj = min(bd, depth), min(bj, weight.shape[1] // 4)
    nd, nj = depth // bd, width // (2 * bj)
    rows_t, rows_c = toks[0].shape[0], cots[0].shape[0]
    tokens = rows_t * ncol
    carry_in = j0 + width < weight.shape[1]
    bf, f32 = jnp.bfloat16, jnp.float32
    hbm = pl.BlockSpec(memory_space=pl.ANY)
    tile_at = lambda d, j, m: (d0 // bd + d, j0 // (2 * bj) + j)
    shape = jax.ShapeDtypeStruct

    def whole(dims, kind):
        return pl.BlockSpec(dims, lambda d, j, m, n=len(dims): (0,) * n), shape(dims, kind)

    extra = [x for x in (wg, out_prev, in_prev) if x is not None]
    outs = [
        (pl.BlockSpec((bd, 2 * bj), tile_at), shape(weight.shape, bf)),
        whole((3, width), f32),
    ]
    if final:
        outs += [whole((rows_c, width), bf)] * nrow + [whole((1, width), f32)]
    else:
        outs += [(hbm, shape((2 * nj, tokens, bj), f32))]
    if carry_in:
        outs += [whole((nd, tokens, bd), f32)]
    else:
        outs += [whole((nz, rows_t, depth), f32), whole((nz, rows_t, depth), bf)]
    n_in = 1 + ncol + nrow + 2
    grid_spec = pltpu.PrefetchScalarGridSpec(
        num_scalar_prefetch=1,
        grid=(nd, nj),
        in_specs=[hbm] * (nrow + ncol)
        + [
            pl.BlockSpec((bd, 2 * bj), tile_at),
            pl.BlockSpec((8, 2 * bj), lambda d, j, m: (0, j0 // (2 * bj) + j)),
        ]
        + [hbm] * len(extra),
        out_specs=[spec for spec, _ in outs],
        scratch_shapes=[
            pltpu.VMEM((nd, tokens, bd), bf),
            pltpu.VMEM((nd, bd, tokens), bf),
            pltpu.VMEM((2 * nj, tokens, bj), bf),
            pltpu.VMEM((2 * nj, tokens, bj), f32),
            pltpu.VMEM((nd, tokens, bd), f32),
            pltpu.VMEM((2 * nj, 3, 8, bj), f32),
            pltpu.VMEM((bd, bj), bf),
            pltpu.VMEM((bd, bj), bf),
            pltpu.VMEM((bd, bj), f32),
            pltpu.VMEM((bd, bj), f32),
            pltpu.SemaphoreType.DMA((2 * nj * nrow + nd * ncol + 1,)),
            pltpu.SemaphoreType.DMA((2 * nj,)),
        ],
    )
    return pl.pallas_call(
        functools.partial(
            main_kernel, nrow=nrow, ncol=ncol, nd=nd, nj=nj, bd=bd, bj=bj, strip=strip, d0=d0, t0=t0,
            j0=j0, carry_out=out_prev is not None, last_out=final, carry_in=carry_in,
        ),
        grid_spec=grid_spec,
        out_shape=[out for _, out in outs],
        input_output_aliases={} if wg is None else {n_in: 0},
        compiler_params=pltpu.CompilerParams(vmem_limit_bytes=63 * 1024 * 1024),
        cost_estimate=pl.CostEstimate(
            flops=20 * depth * width * tokens,
            bytes_accessed=4 * depth * width,
            transcendentals=2 * depth * width,
        ),
        name="main_kernel",
    )(meta, *toks, *cots, weight, consts, *extra)


def swap(value, axis, size, k):
    return lax.ppermute(value, axis, [(i, i ^ k) for i in range(size)])


def gather_cotangent(nrow, mine):
    if nrow != 4:
        return [mine] + [swap(mine, "row", nrow, k) for k in range(1, nrow)]
    one, two = [swap(mine, "row", nrow, k) for k in (1, 2)]
    half = mine.shape[0] // 2
    far = [swap(two[:half], "row", nrow, 1), swap(one[half:], "row", nrow, 2)]
    return [mine, one, two, jnp.concatenate(far, axis=0)]


def layer(nrow, ncol, tokens, weight, logits, cotangent):
    nz = ncol // 2
    f32, bf = jnp.float32, jnp.bfloat16
    depth, width = weight.shape
    cut = depth // 4

    def gather_tokens(t):
        toks = []
        for t in [t] + [swap(t, "col", ncol, 2 * k) for k in range(1, nz)]:
            toks += [t, swap(t, "col", ncol, 1)]
        return toks

    first = gather_tokens(tokens[:, :cut])
    cots = gather_cotangent(nrow, cotangent)
    rest = gather_tokens(tokens[:, cut:])
    peak = jnp.max(jnp.abs(weight), axis=0, keepdims=True).astype(f32)
    for other in [swap(peak, "row", nrow, k) for k in range(1, nrow)]:
        peak = jnp.maximum(peak, other)
    shares = jax.nn.softmax(logits, axis=0)
    spacing = [(peak + EPSILON) / level for level in LEVELS]
    scale = [spacing[n] / (2.0 * TWO_PI) * (1.0, 1.0, -FOLD)[n] for n in range(3)]
    consts = jnp.concatenate(
        [1.0 / spacing[0], 1.0 / spacing[2]]
        + [shares[n : n + 1] * scale[n] for n in range(3)]
        + [shares[0:1] * 0.5, shares[1:2] * 0.5, shares[2:3] * (0.5 * FOLD)],
        axis=0,
    )
    meta = jnp.stack([lax.axis_index("row"), lax.axis_index("col")]).astype(jnp.int32)

    calls = [
        (first, (0, cut), 0, (0, width), False),
        (rest, (cut, 2 * cut), 0, (0, width), False),
        (rest, (3 * cut, cut), 2 * cut, (0, width // 2), True),
        (rest, (3 * cut, cut), 2 * cut, (width // 2, width // 2), True),
    ]
    wg = out_prev = in_prev = None
    parts, commons, mixed, inputs = [], [], [], []
    for toks, rows, t0, cols, final in calls:
        wg, part, *res = main_call(
            meta, toks, cots, weight, consts, wg, out_prev, in_prev, rows=rows, t0=t0, cols=cols, final=final
        )
        parts.append(part)
        if final:
            outs, common, res = res[:nrow], res[nrow], res[nrow + 1 :]
            commons.append(common)
            far = [swap(outs[k], "row", nrow, k) for k in range(1, nrow)]
            mixed.append(sum([outs[0].astype(f32)] + [x.astype(f32) for x in far]).astype(bf))
        else:
            out_prev, res = res[0], res[1:]
        if cols[0] + cols[1] < width:
            in_prev = res[0]
        else:
            keep, send = res
            got = swap(send, "col", ncol, 1)
            sums = [keep[k] + got[k].astype(f32) for k in range(nz)]
            halves = [x.astype(bf) for x in sums]
            far = [swap(halves[k], "col", ncol, 2 * k) for k in range(1, nz)]
            inputs.append(sum([sums[0]] + [x.astype(f32) for x in far]).astype(bf))
    mixed_out = jnp.concatenate(mixed, axis=1)
    input_grad = jnp.concatenate(inputs, axis=1)

    parts = parts[0] + parts[1] + jnp.concatenate(parts[2:], axis=1)
    sines = jnp.concatenate([scale[n] * parts[n : n + 1] for n in range(3)], axis=0)
    common = jnp.concatenate(commons, axis=1) + jnp.sum(shares * sines, axis=0, keepdims=True)
    terms = common - sines
    far = [swap(terms, "row", nrow, k) for k in range(1, nrow)]
    terms = sum([terms] + far)
    logit_grad = shares * (terms - jnp.sum(shares * terms, axis=0, keepdims=True))
    return mixed_out, input_grad, wg, logit_grad


def solution(mesh):
    in_specs = (P("col", "row"), P("row", "col"), P(None, "col"), P("row", "col"))
    out_specs = (P("row", "col"), P("col", "row"), P("row", "col"), P(None, "col"))
    nrow, ncol = mesh.shape["row"], mesh.shape["col"]
    body = functools.partial(layer, nrow, ncol)
    return jax.shard_map(body, mesh=mesh, in_specs=in_specs, out_specs=out_specs, check_vma=False)
```
